32 devices in a mesh: row: 8 (over z, core), col: 4 (over y, x).
Axes of the slice: x: 2, y: 2, z: 4, core: 2. Of those that a mesh axis runs over, the one named last changes fastest.
Arguments:
- surface: bfloat16 [1024, 32768], P(None, 'row'), may hold values from -6 to 6
- block_map: int32 [1024, 32], P(None, 'row'), may hold values 0 or 1
- vectors: bfloat16 [32768, 4096], P('row', 'col'), may hold values from -0.03125 to 0.03125
- poles: bfloat16 [4096], P('col'), may hold values from 2.015625 to 31.875, as said below
- energies: bfloat16 [64], P('col'), may hold values from 2 to 31.75, as said below
Outputs:
- rmatrix: float32 [64, 1024, 1024], P('col', 'row')
The draws below stay inside these ranges and needn't reach their ends.
Inputs may be any that keep to these rules, and one draw needn't show every extreme that they name: `poles`: each pole is 2^j (1 + m/128) with j in 1 to 4 and m odd, exactly as stored; every pole differs from every energy by 1/64 or more. `energies`: each energy is 2^j (1 + m/128) with j in 1 to 4 and m even, exactly as stored.
All inputs are finite; a program needn't handle non-finite values. No bound on the sum of `block_map` on one device may be relied on, other than what follows from the above.
Results may differ from the reference program's by a relative error of at most 0.0042.
Values may be sent and summed in bfloat16 or wider, within the bound.
A program may use at most 64 MiB of HBM per device.

```python
import jax
import jax.numpy as jnp
from jax import lax

NCH = 1024
NPOLE = 4096
NROWS = 32768
NRB = 32
BLOCK = 1024
NE = 64


def lattice(key, salt, length_total, parity, low_end, high_end):
    octave = jax.random.randint(jax.random.fold_in(key, salt), (length_total,), 1, 5)
    offset_index = 2 * jax.random.randint(jax.random.fold_in(key, salt + 1), (length_total,), 0, 64) + parity
    position = jnp.arange(length_total)
    octave = jnp.where(position == 0, 1, jnp.where(position == length_total - 1, 4, octave))
    offset_index = jnp.where(position == 0, low_end, jnp.where(position == length_total - 1, high_end, offset_index))
    octave_scale = jnp.left_shift(jnp.ones_like(octave), octave).astype(jnp.float32)
    return octave_scale * (1.0 + offset_index.astype(jnp.float32) / 128.0)


def draw_poles(key, part):
    return lattice(key, 11, NPOLE, 1, 1, 127).astype(jnp.bfloat16)


def draw_energies(key, part):
    return lattice(key, 23, NE, 0, 0, 126).astype(jnp.bfloat16)


def plant(array, key, smallest, top_value):
    spot = [jax.random.randint(jax.random.fold_in(key, axis), (), 0, length) for axis, length in enumerate(array.shape)]
    longest = array.shape.index(max(array.shape))
    neighbour = spot[:longest] + [(spot[longest] + 1) % array.shape[longest]] + spot[longest + 1:]
    return array.at[tuple(spot)].set(smallest).at[tuple(neighbour)].set(top_value)


def with_spikes(array, own_key, source, target, blocks, factor):
    owner, partner = [(jnp.arange(array.shape[axis_at]) // (array.shape[axis_at] // blocks)).reshape([-1 if axis == axis_at else 1 for axis in range(array.ndim)]) for axis_at in (source, target)]
    chosen = jax.random.permutation(own_key, blocks)[partner]
    strong = (owner == chosen) | (owner == (partner + blocks // 2) % blocks)
    return jnp.where(strong, factor * array, array)


def steps_of(key, shape, split, low, high):
    gain, own = 1.0, jax.random.fold_in(key, 6)
    for dim, parts in split:
        heights = jnp.exp(jax.random.uniform(jax.random.fold_in(own, dim), (parts,), jnp.float32, low / len(split), high / len(split)))
        gain = gain * jnp.repeat(heights, shape[dim] // parts).reshape([-1 if axis == dim else 1 for axis in range(len(shape))])
    return gain


def noise(key, dims, deviation, limit, shards=(), dtype=jnp.bfloat16):
    drawn = deviation * jax.random.normal(key, dims, jnp.float32)
    if shards:
        drawn = drawn * steps_of(key, dims, shards, -0.22, 0.18)
    return jnp.clip(drawn, -limit, limit).astype(dtype)


def heavy_noise(rng, shape, deviation, reach, cuts, heavy, dtype=jnp.bfloat16):
    values = deviation * jax.random.normal(rng, shape, jnp.float32)
    if cuts:
        values = values * steps_of(rng, shape, cuts, -0.22, 0.18)
    return jnp.clip(with_spikes(values, jax.random.fold_in(rng, 3), *heavy), -reach, reach).astype(dtype)


def setup_inputs(seed: int = 0) -> dict:
    arg_keys = jax.random.split(jax.random.key(seed), 6)
    surface = heavy_noise(arg_keys[0], (NCH, NROWS), 1.0, 6.0, ((1, 8),), (1, 0, 8, 2.0))
    block_map = plant((jax.random.randint(arg_keys[1], (NCH, NRB), 0, 2) < 1).astype(jnp.int32), jax.random.fold_in(arg_keys[1], 1), 0, 1)
    vectors = noise(arg_keys[2], (NROWS, NPOLE), NROWS ** -0.5, 0.03125, ((0, 8), (1, 4)))
    poles = draw_poles(jax.random.fold_in(arg_keys[5], 71), 0)
    energies = draw_energies(jax.random.fold_in(arg_keys[5], 71), 0)
    return dict(surface=surface, block_map=block_map, vectors=vectors, poles=poles, energies=energies)


def reference(surface, block_map, vectors, poles, energies):
    keep = jnp.repeat(block_map, BLOCK, axis=1)
    masked = jnp.where(keep == 1, surface, jnp.zeros_like(surface))
    amplitude = jnp.dot(masked, vectors, preferred_element_type=jnp.float32).astype(jnp.bfloat16)
    widened = amplitude.astype(jnp.float32)
    pole_vals = poles.astype(jnp.float32)
    factor = NPOLE ** -0.5

    def single(energy):
        inverse = 1.0 / (pole_vals - energy.astype(jnp.float32))
        scaled = (widened * inverse[None, :]).astype(jnp.bfloat16)
        total = lax.dot_general(scaled, amplitude, (((1,), (1,)), ((), ())), preferred_element_type=jnp.float32)
        return total * factor

    return lax.map(single, energies)
```

```python
import functools

import jax
import jax.numpy as jnp
from jax import lax
from jax.experimental import pallas as pl
from jax.experimental.pallas import tpu as pltpu
from jax.sharding import PartitionSpec as P

NPOLE = 4096
MESH = pl.DeviceIdType.MESH
PARTS = 2


def xor(z, m):
    out, bit = z, 1
    while bit <= m:
        if m & bit:
            out = out + bit - 2 * bit * ((z // bit) % 2)
        bit *= 2
    return out


def kernel(n_row, n_col, en_ref, bm_ref, po_ref, surf_hbm, vec_hbm, out_ref,
           surf, vec, keep_all, pacc, rsib, zsend, zrecv, amp, scaled, poles,
           surf_sem, vec_sem, sib_s, sib_r, rz_s, rz_r, az_s, az_r,
           ring_s, ring_r, core_s, core_r, pol_s, pol_r):
    n_z = n_row // 2
    hops = n_col // 2
    row, col = lax.axis_index("row"), lax.axis_index("col")
    z, core = row // 2, row % 2
    other = 1 - core
    half_y = n_col // 2
    upper = col % 2
    pos = (1 - upper) * (col // 2) + upper * (n_col - 1 - col // 2)

    def col_at(p):
        p = (p + 2 * n_col) % n_col
        high = p // half_y
        return (1 - high) * (2 * p) + high * (2 * (n_col - 1 - p) + 1)

    own = pacc.shape[3]
    pair = 2 * own
    basis = vec.shape[1]
    blocks = vec.shape[0]
    part = pacc.shape[4]
    sibling = (z * 2 + other, col)
    right, left = (row, col_at(pos + 1)), (row, col_at(pos - 1))
    steps = [(f, m) for f in range(PARTS) for m in range(n_z - 1, -1, -1)]
    items = sorted(((f, m) for f in range(PARTS) for m in range(n_z)),
                   key=lambda fm: (fm[1] // 2, fm[0], fm[1] % 2))

    def surf_copy(step):
        zr = xor(z, steps[step][1])
        return pltpu.make_async_copy(
            surf_hbm.at[pl.ds(pl.multiple_of(zr * pair, pair), pair), :],
            surf.at[step % 2], surf_sem.at[step % 2])

    def vec_copy(j):
        return pltpu.make_async_copy(
            vec_hbm.at[pl.ds(j * basis, basis), :], vec.at[j], vec_sem.at[j])

    surf_copy(0).start()
    for j in range(blocks):
        vec_copy(j).start()
    surf_copy(1).start()

    def remote(src, dst, ss, rs, dev):
        return pltpu.make_async_remote_copy(
            src_ref=src, dst_ref=dst, send_sem=ss, recv_sem=rs,
            device_id=dev, device_id_type=MESH)

    barrier = pltpu.get_barrier_semaphore()
    partners = [sibling]
    partners += [(xor(z, m) * 2 + core, col) for m in range(1, n_z)]
    partners += [(row, (col + d) % n_col) for d in range(1, n_col)]
    for dev in partners:
        pl.semaphore_signal(barrier, inc=1, device_id=dev, device_id_type=MESH)

    poles[col] = jnp.broadcast_to(po_ref[...].astype(jnp.float32)[None, :], poles.shape[1:])
    wide_map = jnp.where(bm_ref[...] == 1, 1.0, 0.0)
    wide_map = jnp.concatenate([wide_map, jnp.zeros((8 - blocks, wide_map.shape[1]), jnp.float32)], axis=0)
    keep_all[...] = wide_map.T

    out_ref[...] = jnp.zeros_like(out_ref)

    def dot1(step):
        f, m = steps[step]
        zr = xor(z, m)
        surf_copy(step).wait()
        keep = keep_all[pl.ds(pl.multiple_of(zr * pair, pair), pair), :].astype(jnp.bfloat16)
        for j in range(blocks):
            if step == 0:
                vec_copy(j).wait()
            masked = surf[step % 2, :, j * basis:(j + 1) * basis] * keep[:, j:j + 1]
            term = jnp.dot(masked, vec[j, :, f * part:(f + 1) * part], preferred_element_type=jnp.float32)
            term = term.reshape(2, own, part)
            if j == 0:
                pacc[f, m] = term
            else:
                pacc[f, m] += term
        if step + 2 < len(steps):
            surf_copy(step + 2).start()

    def sib_copy(f, m):
        return remote(pacc.at[f, m, other], rsib.at[f, m], sib_s.at[f, m], sib_r.at[f, m], sibling)

    def rz_copy(f, m):
        return remote(zsend.at[f, m], zrecv.at[f, m], rz_s.at[f, m], rz_r.at[f, m],
                      (xor(z, m) * 2 + core, col))

    def pol_copy(d):
        return remote(poles.at[col], poles.at[col], pol_s.at[d], pol_r.at[d],
                      (row, (col + d) % n_col))

    def pass_on(f, m):
        sib_copy(f, m).wait_recv()
        total = pacc[f, m, core] + rsib[f, m]
        if m == 0:
            pacc[f, m, core] = total
        else:
            zsend[f, m] = total.astype(jnp.bfloat16)
            rz_copy(f, m).start()

    for step in range(len(steps)):
        dot1(step)
        if step == 0:
            pl.semaphore_wait(barrier, len(partners))
        sib_copy(*steps[step]).start()
        if step == 0:
            for d in range(1, n_col):
                pol_copy(d).start()
        if step > 0:
            pass_on(*steps[step - 1])
    pass_on(*steps[-1])

    lower = jnp.minimum(z, n_z - 1 - z)
    mirror = z // (n_z // 2)

    def source(k):
        odd = k % 2
        near = lower + (1 - odd) * (k // 2) - odd * ((k + 1) // 2)
        near = jnp.where(k <= 2 * lower, near, k)
        return (1 - mirror) * near + mirror * (n_z - 1 - near)

    def az_copy(f, zr, way):
        block = amp.at[f, col, zr, core]
        return remote(block, block, az_s.at[f, way, zr], az_r.at[f, zr],
                      ((z + 1 - 2 * way) * 2 + core, col))

    def line(f, m, act):
        zr = source(m)

        @pl.when((zr <= z) & (z < n_z - 1))
        def _():
            act(az_copy(f, zr, 0))

        @pl.when((zr >= z) & (z > 0))
        def _():
            act(az_copy(f, zr, 1))

    def ring_copy(way, h, f, m):
        q = col_at(pos - (h - 1)) if way == 0 else col_at(pos + (h - 1))
        zr = source(m)
        if h == hops:
            block = amp.at[f, q, zr, core, pl.ds(way * (own // 2), own // 2)]
        else:
            block = amp.at[f, q, zr, core]
        return remote(block, block, ring_s.at[f, way, h - 1, m], ring_r.at[f, way, h - 1, m],
                      right if way == 0 else left)

    def core_copy(o, f, m):
        block = amp.at[f, col_at(pos + o), source(m), core]
        return remote(block, block, core_s.at[f, o, m], core_r.at[f, o, m], sibling)

    def finish(f):
        total = pacc[f, 0, core]
        for m in range(n_z - 1, 0, -1):
            rz_copy(f, m).wait_recv()
            total = total + zrecv[f, m].astype(jnp.float32)
        amp[f, col, z, core] = total.astype(jnp.bfloat16)

    def scale(o, f):
        q = col_at(pos + o)

        def one(e, carry):
            gap = poles[q, 0:1, pl.ds(pl.multiple_of(f * part, part), part)] - en_ref[e].astype(jnp.float32)
            inverse = (NPOLE ** -0.5) / gap
            wide = amp[f, q, z, core].astype(jnp.float32)
            scaled[f, o, pl.ds(pl.multiple_of(e * own, own), own), :] = (wide * inverse).astype(jnp.bfloat16)
            return carry

        lax.fori_loop(0, en_ref.shape[0], one, 0)

    def granule(o, f, m):
        q, zr = col_at(pos + o), source(m)
        core_copy(o, f, m).wait_recv()
        cols = pl.ds(pl.multiple_of(zr * pair, pair), pair)
        out_ref[:, cols] += lax.dot_general(
            scaled[f, o], amp[f, q, zr].reshape(pair, part),
            (((1,), (1,)), ((), ())), preferred_element_type=jnp.float32)

    def at(t):
        return (t % (2 * PARTS)) // 2, 2 * (t // (2 * PARTS)) + t % 2

    def held(t):
        return (t >= 0) & (t < len(items))

    def slot(t, carry):
        @pl.when(held(t))
        def _():
            f, m = at(t)

            @pl.when(m == 0)
            def _():
                finish(f)

            @pl.when(m > 0)
            def _():
                az_copy(f, source(m), mirror).wait_recv()

            line(f, m, lambda copy: copy.start())
            ring_copy(0, 1, f, m).start()
            ring_copy(1, 1, f, m).start()
            core_copy(0, f, m).start()

            @pl.when(m == 0)
            def _():
                scale(0, f)

            @pl.when(t == 0)
            def _():
                for d in range(1, n_col):
                    pol_copy(d).wait_recv()

        for h in range(1, hops + 1):
            @pl.when(held(t - h))
            def _():
                f, m = at(t - h)
                ring_copy(0, h, f, m).wait_recv()
                if h < hops:
                    ring_copy(0, h + 1, f, m).start()
                    core_copy(n_col - h, f, m).start()
                ring_copy(1, h, f, m).wait_recv()
                if h < hops:
                    ring_copy(1, h + 1, f, m).start()
                core_copy(h, f, m).start()

                @pl.when(m == 0)
                def _():
                    scale(h, f)
                    if h < hops:
                        scale(n_col - h, f)

        def one(o, carry):
            i = t - 1 - jnp.minimum(o, n_col - o)

            @pl.when(held(i))
            def _():
                granule(o, *at(i))

            return carry

        lax.fori_loop(0, n_col, one, 0)
        return carry

    lax.fori_loop(0, len(items) + hops + 1, slot, 0)

    for f, m in items:
        sib_copy(f, m).wait_send()
        if m > 0:
            rz_copy(f, m).wait_send()
        line(f, m, lambda copy: copy.wait_send())
        for o in range(n_col):
            core_copy(o, f, m).wait_send()
        for h in range(1, hops + 1):
            ring_copy(0, h, f, m).wait_send()
            ring_copy(1, h, f, m).wait_send()
    for d in range(1, n_col):
        pol_copy(d).wait_send()


def body(surface, block_map, vectors, poles, energies):
    n_row, n_col = lax.axis_size("row"), lax.axis_size("col")
    n_z, hops = n_row // 2, n_col // 2
    chans, depth = surface.shape
    own = chans // n_row
    blocks = block_map.shape[1]
    basis = depth // blocks
    per = vectors.shape[1]
    part = per // PARTS
    e_count = energies.shape[0]
    dma = pltpu.SemaphoreType.DMA
    vmem = pl.BlockSpec(memory_space=pltpu.VMEM)
    hbm = pl.BlockSpec(memory_space=pl.ANY)
    out = pl.pallas_call(
        functools.partial(kernel, n_row, n_col),
        out_shape=pltpu.VMEM((e_count * own, chans), jnp.float32),
        in_specs=[pl.BlockSpec(memory_space=pltpu.SMEM), vmem, vmem, hbm, hbm],
        out_specs=vmem,
        scratch_shapes=[
            pltpu.VMEM((2, 2 * own, depth), jnp.bfloat16),
            pltpu.VMEM((blocks, basis, per), jnp.bfloat16),
            pltpu.VMEM((chans, 8), jnp.float32),
            pltpu.VMEM((PARTS, n_z, 2, own, part), jnp.float32),
            pltpu.VMEM((PARTS, n_z, own, part), jnp.float32),
            pltpu.VMEM((PARTS, n_z, own, part), jnp.bfloat16),
            pltpu.VMEM((PARTS, n_z, own, part), jnp.bfloat16),
            pltpu.VMEM((PARTS, n_col, n_z, 2, own, part), jnp.bfloat16),
            pltpu.VMEM((PARTS, n_col, e_count * own, part), jnp.bfloat16),
            pltpu.VMEM((n_col, 8, per), jnp.float32),
            dma((2,)), dma((blocks,)),
            *[dma((PARTS, n_z))] * 4,
            dma((PARTS, 2, n_z)), dma((PARTS, n_z)),
            dma((PARTS, 2, hops, n_z)), dma((PARTS, 2, hops, n_z)),
            dma((PARTS, n_col, n_z)), dma((PARTS, n_col, n_z)),
            dma((n_col,)), dma((n_col,)),
        ],
        compiler_params=pltpu.CompilerParams(
            collective_id=0, has_side_effects=True, vmem_limit_bytes=54 * 1024 * 1024),
    )(energies, block_map.T, poles, surface, vectors)
    return out.reshape(e_count, own, chans)


def solution(mesh):
    placed = (P(None, "row"), P(None, "row"), P("row", "col"), P("col"), P("col"))
    return jax.shard_map(
        body, mesh=mesh, in_specs=placed, out_specs=P("col", "row", None), check_vma=False
    )
```

```python
import functools

import jax
import jax.numpy as jnp
from jax import lax
from jax.experimental import pallas as pl
from jax.experimental.pallas import tpu as pltpu
from jax.sharding import PartitionSpec as P

NPOLE = 4096
MESH = pl.DeviceIdType.MESH
PARTS = 2
LAG = 2


def xor(z, m):
    out, bit = z, 1
    while bit <= m:
        if m & bit:
            out = out + bit - 2 * bit * ((z // bit) % 2)
        bit *= 2
    return out


def kernel(n_row, n_col, en_ref, bm_ref, po_ref, surf_hbm, vec_hbm, out_ref,
           surf, vec, keep_all, pacc, rsib, zsend, zrecv, amp, scaled, poles,
           surf_sem, vec_sem, sib_s, sib_r, rz_s, rz_r, az_s, az_r,
           ring_s, ring_r, core_s, core_r, pol_s, pol_r):
    n_z = n_row // 2
    hops = n_col // 2
    row, col = lax.axis_index("row"), lax.axis_index("col")
    z, core = row // 2, row % 2
    other = 1 - core
    half_y = n_col // 2
    upper = col % 2
    pos = (1 - upper) * (col // 2) + upper * (n_col - 1 - col // 2)

    def col_at(p):
        p = (p + 2 * n_col) % n_col
        high = p // half_y
        return (1 - high) * (2 * p) + high * (2 * (n_col - 1 - p) + 1)

    own = pacc.shape[3]
    pair = 2 * own
    basis = vec.shape[1]
    blocks = vec.shape[0]
    part = pacc.shape[4]
    sibling = (z * 2 + other, col)
    right, left = (row, col_at(pos + 1)), (row, col_at(pos - 1))
    steps = [(f, m) for f in range(PARTS) for m in range(n_z - 1, -1, -1)]
    items = sorted(((f, m) for f in range(PARTS) for m in range(n_z)),
                   key=lambda fm: (fm[1] // 2, fm[0], fm[1] % 2))

    def surf_copy(step):
        zr = xor(z, steps[step][1])
        return pltpu.make_async_copy(
            surf_hbm.at[pl.ds(pl.multiple_of(zr * pair, pair), pair), :],
            surf.at[step % 2], surf_sem.at[step % 2])

    def vec_copy(j):
        return pltpu.make_async_copy(
            vec_hbm.at[pl.ds(j * basis, basis), :], vec.at[j], vec_sem.at[j])

    surf_copy(0).start()
    for j in range(blocks):
        vec_copy(j).start()
    surf_copy(1).start()

    def remote(src, dst, ss, rs, dev):
        return pltpu.make_async_remote_copy(
            src_ref=src, dst_ref=dst, send_sem=ss, recv_sem=rs,
            device_id=dev, device_id_type=MESH)

    barrier = pltpu.get_barrier_semaphore()
    partners = [sibling]
    partners += [(xor(z, m) * 2 + core, col) for m in range(1, n_z)]
    partners += [(row, (col + d) % n_col) for d in range(1, n_col)]
    for dev in partners:
        pl.semaphore_signal(barrier, inc=1, device_id=dev, device_id_type=MESH)

    poles[col] = jnp.broadcast_to(po_ref[...].astype(jnp.float32)[None, :], poles.shape[1:])
    wide_map = jnp.where(bm_ref[...] == 1, 1.0, 0.0)
    wide_map = jnp.concatenate([wide_map, jnp.zeros((8 - blocks, wide_map.shape[1]), jnp.float32)], axis=0)
    keep_all[...] = wide_map.T

    out_ref[...] = jnp.zeros_like(out_ref)

    def dot1(step):
        f, m = steps[step]
        zr = xor(z, m)
        surf_copy(step).wait()
        keep = keep_all[pl.ds(pl.multiple_of(zr * pair, pair), pair), :].astype(jnp.bfloat16)
        for j in range(blocks):
            if step == 0:
                vec_copy(j).wait()
            masked = surf[step % 2, :, j * basis:(j + 1) * basis] * keep[:, j:j + 1]
            term = jnp.dot(masked, vec[j, :, f * part:(f + 1) * part], preferred_element_type=jnp.float32)
            term = term.reshape(2, own, part)
            if j == 0:
                pacc[f, m] = term
            else:
                pacc[f, m] += term
        if step + 2 < len(steps):
            surf_copy(step + 2).start()

    def sib_copy(f, m):
        return remote(pacc.at[f, m, other], rsib.at[f, m], sib_s.at[f, m], sib_r.at[f, m], sibling)

    def rz_copy(f, m):
        return remote(zsend.at[f, m], zrecv.at[f, m], rz_s.at[f, m], rz_r.at[f, m],
                      (xor(z, m) * 2 + core, col))

    def pol_copy(d):
        return remote(poles.at[col], poles.at[col], pol_s.at[d], pol_r.at[d],
                      (row, (col + d) % n_col))

    def pass_on(f, m):
        sib_copy(f, m).wait_recv()
        total = pacc[f, m, core] + rsib[f, m]
        if m == 0:
            pacc[f, m, core] = total
        else:
            zsend[f, m] = total.astype(jnp.bfloat16)
            rz_copy(f, m).start()

    for step in range(len(steps)):
        dot1(step)
        if step == 0:
            pl.semaphore_wait(barrier, len(partners))
        sib_copy(*steps[step]).start()
        if step == 0:
            for d in range(1, n_col):
                pol_copy(d).start()
        if step > 0:
            pass_on(*steps[step - 1])
    pass_on(*steps[-1])

    lower = jnp.minimum(z, n_z - 1 - z)
    mirror = z // (n_z // 2)

    def source(k):
        odd = k % 2
        near = lower + (1 - odd) * (k // 2) - odd * ((k + 1) // 2)
        near = jnp.where(k <= 2 * lower, near, k)
        return (1 - mirror) * near + mirror * (n_z - 1 - near)

    def az_copy(f, zr, way):
        block = amp.at[f, col, zr, core]
        return remote(block, block, az_s.at[f, way, zr], az_r.at[f, zr],
                      ((z + 1 - 2 * way) * 2 + core, col))

    def line(f, m, act):
        zr = source(m)

        @pl.when((zr <= z) & (z < n_z - 1))
        def _():
            act(az_copy(f, zr, 0))

        @pl.when((zr >= z) & (z > 0))
        def _():
            act(az_copy(f, zr, 1))

    def ring_copy(way, h, f, m):
        q = col_at(pos - (h - 1)) if way == 0 else col_at(pos + (h - 1))
        zr = source(m)
        if h == hops:
            block = amp.at[f, q, zr, core, pl.ds(way * (own // 2), own // 2)]
        else:
            block = amp.at[f, q, zr, core]
        return remote(block, block, ring_s.at[f, way, h - 1, m], ring_r.at[f, way, h - 1, m],
                      right if way == 0 else left)

    def core_copy(o, f, m):
        block = amp.at[f, col_at(pos + o), source(m), core]
        return remote(block, block, core_s.at[f, o, m], core_r.at[f, o, m], sibling)

    def finish(f):
        total = pacc[f, 0, core]
        for m in range(n_z - 1, 0, -1):
            rz_copy(f, m).wait_recv()
            total = total + zrecv[f, m].astype(jnp.float32)
        amp[f, col, z, core] = total.astype(jnp.bfloat16)

    def scale(o, f):
        q = col_at(pos + o)

        def one(e, carry):
            gap = poles[q, 0:1, pl.ds(pl.multiple_of(f * part, part), part)] - en_ref[e].astype(jnp.float32)
            inverse = (NPOLE ** -0.5) / gap
            wide = amp[f, q, z, core].astype(jnp.float32)
            scaled[f, o, pl.ds(pl.multiple_of(e * own, own), own), :] = (wide * inverse).astype(jnp.bfloat16)
            return carry

        lax.fori_loop(0, en_ref.shape[0], one, 0)

    def granule(o, f, m):
        q, zr = col_at(pos + o), source(m)
        core_copy(o, f, m).wait_recv()
        cols = pl.ds(pl.multiple_of(zr * pair, pair), pair)
        out_ref[:, cols] += lax.dot_general(
            scaled[f, o], amp[f, q, zr].reshape(pair, part),
            (((1,), (1,)), ((), ())), preferred_element_type=jnp.float32)

    def at(t):
        return (t % (2 * PARTS)) // 2, 2 * (t // (2 * PARTS)) + t % 2

    def held(t):
        return (t >= 0) & (t < len(items))

    def slot(t, carry):
        @pl.when(held(t))
        def _():
            f, m = at(t)

            @pl.when(m == 0)
            def _():
                finish(f)

            @pl.when(m > 0)
            def _():
                az_copy(f, source(m), mirror).wait_recv()

            line(f, m, lambda copy: copy.start())
            ring_copy(0, 1, f, m).start()
            ring_copy(1, 1, f, m).start()
            core_copy(0, f, m).start()

            @pl.when(m == 0)
            def _():
                scale(0, f)

            @pl.when(t == 0)
            def _():
                for d in range(1, n_col):
                    pol_copy(d).wait_recv()

        for h in range(1, hops + 1):
            @pl.when(held(t - LAG * h))
            def _():
                f, m = at(t - LAG * h)
                ring_copy(0, h, f, m).wait_recv()
                if h < hops:
                    ring_copy(0, h + 1, f, m).start()
                    core_copy(n_col - h, f, m).start()
                ring_copy(1, h, f, m).wait_recv()
                if h < hops:
                    ring_copy(1, h + 1, f, m).start()
                core_copy(h, f, m).start()

                @pl.when(m == 0)
                def _():
                    scale(h, f)
                    if h < hops:
                        scale(n_col - h, f)

        def one(o, carry):
            i = t - 1 - LAG * jnp.minimum(o, n_col - o)

            @pl.when(held(i))
            def _():
                granule(o, *at(i))

            return carry

        lax.fori_loop(0, n_col, one, 0)
        return carry

    lax.fori_loop(0, len(items) + LAG * hops + 1, slot, 0)

    for f, m in items:
        sib_copy(f, m).wait_send()
        if m > 0:
            rz_copy(f, m).wait_send()
        line(f, m, lambda copy: copy.wait_send())
        for o in range(n_col):
            core_copy(o, f, m).wait_send()
        for h in range(1, hops + 1):
            ring_copy(0, h, f, m).wait_send()
            ring_copy(1, h, f, m).wait_send()
    for d in range(1, n_col):
        pol_copy(d).wait_send()


def body(surface, block_map, vectors, poles, energies):
    n_row, n_col = lax.axis_size("row"), lax.axis_size("col")
    n_z, hops = n_row // 2, n_col // 2
    chans, depth = surface.shape
    own = chans // n_row
    blocks = block_map.shape[1]
    basis = depth // blocks
    per = vectors.shape[1]
    part = per // PARTS
    e_count = energies.shape[0]
    dma = pltpu.SemaphoreType.DMA
    vmem = pl.BlockSpec(memory_space=pltpu.VMEM)
    hbm = pl.BlockSpec(memory_space=pl.ANY)
    out = pl.pallas_call(
        functools.partial(kernel, n_row, n_col),
        out_shape=pltpu.VMEM((e_count * own, chans), jnp.float32),
        in_specs=[pl.BlockSpec(memory_space=pltpu.SMEM), vmem, vmem, hbm, hbm],
        out_specs=vmem,
        scratch_shapes=[
            pltpu.VMEM((2, 2 * own, depth), jnp.bfloat16),
            pltpu.VMEM((blocks, basis, per), jnp.bfloat16),
            pltpu.VMEM((chans, 8), jnp.float32),
            pltpu.VMEM((PARTS, n_z, 2, own, part), jnp.float32),
            pltpu.VMEM((PARTS, n_z, own, part), jnp.float32),
            pltpu.VMEM((PARTS, n_z, own, part), jnp.bfloat16),
            pltpu.VMEM((PARTS, n_z, own, part), jnp.bfloat16),
            pltpu.VMEM((PARTS, n_col, n_z, 2, own, part), jnp.bfloat16),
            pltpu.VMEM((PARTS, n_col, e_count * own, part), jnp.bfloat16),
            pltpu.VMEM((n_col, 8, per), jnp.float32),
            dma((2,)), dma((blocks,)),
            *[dma((PARTS, n_z))] * 4,
            dma((PARTS, 2, n_z)), dma((PARTS, n_z)),
            dma((PARTS, 2, hops, n_z)), dma((PARTS, 2, hops, n_z)),
            dma((PARTS, n_col, n_z)), dma((PARTS, n_col, n_z)),
            dma((n_col,)), dma((n_col,)),
        ],
        compiler_params=pltpu.CompilerParams(
            collective_id=0, has_side_effects=True, vmem_limit_bytes=54 * 1024 * 1024),
    )(energies, block_map.T, poles, surface, vectors)
    return out.reshape(e_count, own, chans)


def solution(mesh):
    placed = (P(None, "row"), P(None, "row"), P("row", "col"), P("col"), P("col"))
    return jax.shard_map(
        body, mesh=mesh, in_specs=placed, out_specs=P("col", "row", None), check_vma=False
    )
```

```python
import functools

import jax
import jax.numpy as jnp
from jax import lax
from jax.experimental import pallas as pl
from jax.experimental.pallas import tpu as pltpu
from jax.sharding import PartitionSpec as P

NPOLE = 4096
MESH = pl.DeviceIdType.MESH
PARTS = 2


def xor(z, m):
    out, bit = z, 1
    while bit <= m:
        if m & bit:
            out = out + bit - 2 * bit * ((z // bit) % 2)
        bit *= 2
    return out


def kernel(n_row, n_col, en_ref, bm_ref, po_ref, surf_hbm, vec_hbm, out_ref,
           surf, vec, keep_all, pacc, rsib, zsend, zrecv, amp, scaled, poles,
           surf_sem, vec_sem, sib_s, sib_r, rz_s, rz_r, az_s, az_r,
           ring_s, ring_r, core_s, core_r, pol_s, pol_r):
    n_z = n_row // 2
    hops = n_col // 2
    row, col = lax.axis_index("row"), lax.axis_index("col")
    z, core = row // 2, row % 2
    other = 1 - core
    half_y = n_col // 2
    upper = col % 2
    pos = (1 - upper) * (col // 2) + upper * (n_col - 1 - col // 2)

    def col_at(p):
        p = (p + 2 * n_col) % n_col
        high = p // half_y
        return (1 - high) * (2 * p) + high * (2 * (n_col - 1 - p) + 1)

    own = pacc.shape[3]
    pair = 2 * own
    basis = vec.shape[1]
    blocks = vec.shape[0]
    part = pacc.shape[4]
    sibling = (z * 2 + other, col)
    right, left = (row, col_at(pos + 1)), (row, col_at(pos - 1))
    steps = [(f, m) for f in range(PARTS) for m in range(n_z - 1, -1, -1)]
    items = sorted(((f, m) for f in range(PARTS) for m in range(n_z)),
                   key=lambda fm: (fm[1] // 2, fm[0], fm[1] % 2))

    def surf_copy(step):
        zr = xor(z, steps[step][1])
        return pltpu.make_async_copy(
            surf_hbm.at[pl.ds(pl.multiple_of(zr * pair, pair), pair), :],
            surf.at[step % 2], surf_sem.at[step % 2])

    def vec_copy(j):
        return pltpu.make_async_copy(
            vec_hbm.at[pl.ds(j * basis, basis), :], vec.at[j], vec_sem.at[j])

    surf_copy(0).start()
    for j in range(blocks):
        vec_copy(j).start()
    surf_copy(1).start()

    def remote(src, dst, ss, rs, dev):
        return pltpu.make_async_remote_copy(
            src_ref=src, dst_ref=dst, send_sem=ss, recv_sem=rs,
            device_id=dev, device_id_type=MESH)

    barrier = pltpu.get_barrier_semaphore()
    partners = [sibling]
    partners += [(xor(z, m) * 2 + core, col) for m in range(1, n_z)]
    partners += [(row, (col + d) % n_col) for d in range(1, n_col)]
    for dev in partners:
        pl.semaphore_signal(barrier, inc=1, device_id=dev, device_id_type=MESH)

    poles[col] = jnp.broadcast_to(po_ref[...].astype(jnp.float32)[None, :], poles.shape[1:])
    wide_map = jnp.where(bm_ref[...] == 1, 1.0, 0.0)
    wide_map = jnp.concatenate([wide_map, jnp.zeros((8 - blocks, wide_map.shape[1]), jnp.float32)], axis=0)
    keep_all[...] = wide_map.T

    out_ref[...] = jnp.zeros_like(out_ref)

    def dot1(step):
        f, m = steps[step]
        zr = xor(z, m)
        surf_copy(step).wait()
        keep = keep_all[pl.ds(pl.multiple_of(zr * pair, pair), pair), :].astype(jnp.bfloat16)
        for j in range(blocks):
            if step == 0:
                vec_copy(j).wait()
            masked = surf[step % 2, :, j * basis:(j + 1) * basis] * keep[:, j:j + 1]
            term = jnp.dot(masked, vec[j, :, f * part:(f + 1) * part], preferred_element_type=jnp.float32)
            term = term.reshape(2, own, part)
            if j == 0:
                pacc[f, m] = term
            else:
                pacc[f, m] += term
        if step + 2 < len(steps):
            surf_copy(step + 2).start()

    def sib_copy(f, m):
        return remote(pacc.at[f, m, other], rsib.at[f, m], sib_s.at[f, m], sib_r.at[f, m], sibling)

    def rz_copy(f, m):
        return remote(zsend.at[f, m], zrecv.at[f, m], rz_s.at[f, m], rz_r.at[f, m],
                      (xor(z, m) * 2 + core, col))

    def pol_copy(d):
        return remote(poles.at[col], poles.at[col], pol_s.at[d], pol_r.at[d],
                      (row, (col + d) % n_col))

    def pass_on(f, m):
        sib_copy(f, m).wait_recv()
        total = pacc[f, m, core] + rsib[f, m]
        if m == 0:
            pacc[f, m, core] = total
        else:
            zsend[f, m] = total.astype(jnp.bfloat16)
            rz_copy(f, m).start()

    for step in range(len(steps)):
        dot1(step)
        if step == 0:
            pl.semaphore_wait(barrier, len(partners))
        sib_copy(*steps[step]).start()
        if step == 0:
            for d in range(1, n_col):
                pol_copy(d).start()
        if step > 0:
            pass_on(*steps[step - 1])
    pass_on(*steps[-1])

    lower = jnp.minimum(z, n_z - 1 - z)
    mirror = z // (n_z // 2)

    def source(k):
        odd = k % 2
        near = lower + (1 - odd) * (k // 2) - odd * ((k + 1) // 2)
        near = jnp.where(k <= 2 * lower, near, k)
        return (1 - mirror) * near + mirror * (n_z - 1 - near)

    def az_copy(f, zr, way):
        block = amp.at[f, col, zr, core]
        return remote(block, block, az_s.at[f, way, zr], az_r.at[f, zr],
                      ((z + 1 - 2 * way) * 2 + core, col))

    def line(f, m, act):
        zr = source(m)

        @pl.when((zr <= z) & (z < n_z - 1))
        def _():
            act(az_copy(f, zr, 0))

        @pl.when((zr >= z) & (z > 0))
        def _():
            act(az_copy(f, zr, 1))

    def ring_copy(way, h, f, m):
        q = col_at(pos - (h - 1)) if way == 0 else col_at(pos + (h - 1))
        zr = source(m)
        if h == hops:
            block = amp.at[f, q, zr, core, pl.ds(way * (own // 2), own // 2)]
        else:
            block = amp.at[f, q, zr, core]
        return remote(block, block, ring_s.at[f, way, h - 1, m], ring_r.at[f, way, h - 1, m],
                      right if way == 0 else left)

    def core_copy(o, f, m):
        block = amp.at[f, col_at(pos + o), source(m), core]
        return remote(block, block, core_s.at[f, o, m], core_r.at[f, o, m], sibling)

    def finish(f):
        total = pacc[f, 0, core]
        for m in range(n_z - 1, 0, -1):
            rz_copy(f, m).wait_recv()
            total = total + zrecv[f, m].astype(jnp.float32)
        amp[f, col, z, core] = total.astype(jnp.bfloat16)

    def scale(o, f):
        q = col_at(pos + o)

        def one(e, carry):
            gap = poles[q, 0:1, pl.ds(pl.multiple_of(f * part, part), part)] - en_ref[e].astype(jnp.float32)
            inverse = (NPOLE ** -0.5) / gap
            wide = amp[f, q, z, core].astype(jnp.float32)
            scaled[f, o, pl.ds(pl.multiple_of(e * own, own), own), :] = (wide * inverse).astype(jnp.bfloat16)
            return carry

        lax.fori_loop(0, en_ref.shape[0], one, 0)

    def granule(o, f, m):
        q, zr = col_at(pos + o), source(m)
        core_copy(o, f, m).wait_recv()
        cols = pl.ds(pl.multiple_of(zr * pair, pair), pair)
        out_ref[:, cols] += lax.dot_general(
            scaled[f, o], amp[f, q, zr].reshape(pair, part),
            (((1,), (1,)), ((), ())), preferred_element_type=jnp.float32)

    def at(t):
        return (t % (2 * PARTS)) // 2, 2 * (t // (2 * PARTS)) + t % 2

    def held(t):
        return (t >= 0) & (t < len(items))

    def slot(t, carry):
        @pl.when(held(t))
        def _():
            f, m = at(t)

            @pl.when(m == 0)
            def _():
                finish(f)

            @pl.when(m > 0)
            def _():
                az_copy(f, source(m), mirror).wait_recv()

            line(f, m, lambda copy: copy.start())
            ring_copy(0, 1, f, m).start()
            ring_copy(1, 1, f, m).start()
            core_copy(0, f, m).start()

            @pl.when(m == 0)
            def _():
                scale(0, f)

            @pl.when(t == 0)
            def _():
                for d in range(1, n_col):
                    pol_copy(d).wait_recv()

        for h in range(1, hops + 1):
            @pl.when(held(t - h - 1))
            def _():
                f, m = at(t - h - 1)
                ring_copy(0, h, f, m).wait_recv()
                if h < hops:
                    ring_copy(0, h + 1, f, m).start()
                    core_copy(n_col - h, f, m).start()
                ring_copy(1, h, f, m).wait_recv()
                if h < hops:
                    ring_copy(1, h + 1, f, m).start()
                core_copy(h, f, m).start()

                @pl.when(m == 0)
                def _():
                    scale(h, f)
                    if h < hops:
                        scale(n_col - h, f)

        def one(o, carry):
            i = t - 1 - jnp.minimum(o, n_col - o) - jnp.minimum(o, 1)

            @pl.when(held(i))
            def _():
                granule(o, *at(i))

            return carry

        lax.fori_loop(0, n_col, one, 0)
        return carry

    lax.fori_loop(0, len(items) + hops + 2, slot, 0)

    for f, m in items:
        sib_copy(f, m).wait_send()
        if m > 0:
            rz_copy(f, m).wait_send()
        line(f, m, lambda copy: copy.wait_send())
        for o in range(n_col):
            core_copy(o, f, m).wait_send()
        for h in range(1, hops + 1):
            ring_copy(0, h, f, m).wait_send()
            ring_copy(1, h, f, m).wait_send()
    for d in range(1, n_col):
        pol_copy(d).wait_send()


def body(surface, block_map, vectors, poles, energies):
    n_row, n_col = lax.axis_size("row"), lax.axis_size("col")
    n_z, hops = n_row // 2, n_col // 2
    chans, depth = surface.shape
    own = chans // n_row
    blocks = block_map.shape[1]
    basis = depth // blocks
    per = vectors.shape[1]
    part = per // PARTS
    e_count = energies.shape[0]
    dma = pltpu.SemaphoreType.DMA
    vmem = pl.BlockSpec(memory_space=pltpu.VMEM)
    hbm = pl.BlockSpec(memory_space=pl.ANY)
    out = pl.pallas_call(
        functools.partial(kernel, n_row, n_col),
        out_shape=pltpu.VMEM((e_count * own, chans), jnp.float32),
        in_specs=[pl.BlockSpec(memory_space=pltpu.SMEM), vmem, vmem, hbm, hbm],
        out_specs=vmem,
        scratch_shapes=[
            pltpu.VMEM((2, 2 * own, depth), jnp.bfloat16),
            pltpu.VMEM((blocks, basis, per), jnp.bfloat16),
            pltpu.VMEM((chans, 8), jnp.float32),
            pltpu.VMEM((PARTS, n_z, 2, own, part), jnp.float32),
            pltpu.VMEM((PARTS, n_z, own, part), jnp.float32),
            pltpu.VMEM((PARTS, n_z, own, part), jnp.bfloat16),
            pltpu.VMEM((PARTS, n_z, own, part), jnp.bfloat16),
            pltpu.VMEM((PARTS, n_col, n_z, 2, own, part), jnp.bfloat16),
            pltpu.VMEM((PARTS, n_col, e_count * own, part), jnp.bfloat16),
            pltpu.VMEM((n_col, 8, per), jnp.float32),
            dma((2,)), dma((blocks,)),
            *[dma((PARTS, n_z))] * 4,
            dma((PARTS, 2, n_z)), dma((PARTS, n_z)),
            dma((PARTS, 2, hops, n_z)), dma((PARTS, 2, hops, n_z)),
            dma((PARTS, n_col, n_z)), dma((PARTS, n_col, n_z)),
            dma((n_col,)), dma((n_col,)),
        ],
        compiler_params=pltpu.CompilerParams(
            collective_id=0, has_side_effects=True, vmem_limit_bytes=54 * 1024 * 1024),
    )(energies, block_map.T, poles, surface, vectors)
    return out.reshape(e_count, own, chans)


def solution(mesh):
    placed = (P(None, "row"), P(None, "row"), P("row", "col"), P("col"), P("col"))
    return jax.shard_map(
        body, mesh=mesh, in_specs=placed, out_specs=P("col", "row", None), check_vma=False
    )
```
